32 devices in a mesh: blk: 16 (over z, y, core), user: 2 (over x).
Axes of the slice: x: 2, y: 2, z: 4, core: 2. Of those that a mesh axis runs over, the one named last changes fastest.
Arguments:
- user_factors: float32 [16384, 128], P(('blk', 'user')), may hold values from -1.8 to 1.8
- item_factors: float32 [4096, 128], P(('blk', 'user')), may hold values from -1.8 to 1.8
- ratings: bfloat16 [3, 16384, 256], P(None, ('blk', 'user')), may hold values from -4 to 4
- tile_pattern: int32 [3, 128, 2], P(None, ('blk', 'user')), may hold values 0 or 1
- tile_scale: float32 [3, 128, 2], P(None, ('blk', 'user')), may hold values from 0.35 to 4.5
Outputs:
- users_out: float32 [16384, 128], P(('blk', 'user'))
- items_out: float32 [4096, 128], P(('blk', 'user'))
The draws below stay inside these ranges and needn't reach their ends.
All inputs are finite; a program needn't handle non-finite values. No bound on the sum of `tile_pattern` on one device may be relied on, other than what follows from the above.
Results may differ from the reference program's by a relative error of at most 0.0023.
Values may be sent and summed in bfloat16 or wider, within the bound.
A program may use at most 64 MiB of HBM per device.

```python
import jax
import jax.numpy as jnp
from jax import lax

R = 128
TILE = 128
U_DEV = 512
SUB = 3
ITEM_BLK = 256
USERS = 16384
ITEMS = 4096
N_BLK = 16
N_USER = 2


def draw_tile_scale(key, part):
    rows = USERS // TILE
    cols = ITEM_BLK // TILE
    position = jnp.arange(rows, dtype=jnp.float32) / max(rows - 1, 1)
    rising = jnp.exp(jnp.log(3.0) * position)
    random_part = jnp.exp(jax.random.uniform(key, (SUB, rows, cols), jnp.float32, jnp.log(0.5), jnp.log(1.5)))
    return (random_part * rising[None, :, None]).astype(jnp.float32)


def place_ends(drawn, rng, least, high):
    place = [jax.random.randint(jax.random.fold_in(rng, axis), (), 0, length) for axis, length in enumerate(drawn.shape)]
    longest = drawn.shape.index(max(drawn.shape))
    beside = place[:longest] + [(place[longest] + 1) % drawn.shape[longest]] + place[longest + 1:]
    return drawn.at[tuple(place)].set(least).at[tuple(beside)].set(high)


def steps_of(key, dims, pieces, low, largest):
    gain = 1.0
    for dim, parts in pieces:
        draws = jax.random.uniform(jax.random.fold_in(jax.random.fold_in(key, 6), dim), (parts,), jnp.float32, low / len(pieces), largest / len(pieces))
        gain = gain * jnp.repeat(jnp.exp(draws), dims[dim] // parts).reshape((-1,) + (1,) * (len(dims) - 1 - dim))
    return gain


def gaussian(stream_key, dims, width, most, split=(), held_as=jnp.bfloat16):
    result = width * jax.random.normal(stream_key, dims, jnp.float32)
    if split:
        result = result * steps_of(stream_key, dims, split, -0.22, 0.18)
    return jnp.clip(result, -most, most).astype(held_as)


def setup_inputs(seed: int = 0) -> dict:
    key_of = jax.random.split(jax.random.key(seed), 6)
    user_factors = gaussian(key_of[0], (USERS, R), 0.3, 1.8, ((0, 32),), jnp.float32)
    item_factors = gaussian(key_of[1], (ITEMS, R), 0.3, 1.8, ((0, 32),), jnp.float32)
    ratings = gaussian(key_of[2], (SUB, USERS, ITEM_BLK), 1.0, 4.0, ((1, 32),))
    tile_pattern = place_ends((jax.random.randint(key_of[3], (SUB, USERS // TILE, ITEM_BLK // TILE), 0, 4) < 1).astype(jnp.int32), jax.random.fold_in(key_of[3], 1), 0, 1)
    tile_scale = draw_tile_scale(jax.random.fold_in(key_of[5], 71), 0)
    return dict(user_factors=user_factors, item_factors=item_factors, ratings=ratings, tile_pattern=tile_pattern, tile_scale=tile_scale)


penalty = 0.05
user_step = 0.01
item_step = 0.05
epsilon = 1e-06

def local_pass(users, items_low, rating, pattern, scale, tile):
    rows = rating.shape[0]
    cols = rating.shape[1]
    target = rating.astype(jnp.float32).reshape(rows // tile, tile, cols // tile, tile) * scale[:, None, :, None]
    weight = pattern.astype(jnp.float32)[:, None, :, None]

    def errors(factors):
        low = factors.astype(jnp.bfloat16)
        predicted = jnp.dot(low, items_low.T, preferred_element_type=jnp.float32)
        predicted = predicted.reshape(rows // tile, tile, cols // tile, tile)
        return ((weight * (predicted - target)).astype(jnp.bfloat16).reshape(rows, cols), low)
    first_err, first_low = errors(users)
    grad_users = jnp.dot(first_err, items_low, preferred_element_type=jnp.float32) + penalty * users
    users = users - user_step * grad_users
    second_err, second_low = errors(users)
    partial_value = jnp.dot(second_err.T, second_low, preferred_element_type=jnp.float32)
    tile_counts = tile * lax.optimization_barrier(jnp.sum(pattern.astype(jnp.float32), axis=0))
    counts = jnp.broadcast_to(tile_counts[:, None], (cols // tile, tile)).reshape(cols)
    return (users, partial_value, counts)

def reference(user_factors, item_factors, ratings, tile_pattern, tile_scale):
    groups = N_BLK
    group_users = U_DEV * N_USER
    users = user_factors.reshape(groups, group_users, R)
    block = item_factors.reshape(groups, ITEM_BLK, R)
    for section in range(SUB):
        rating = ratings[section].reshape(groups, group_users, ITEM_BLK)
        pattern = tile_pattern[section].reshape(groups, group_users // TILE, ITEM_BLK // TILE)
        scale = tile_scale[section].reshape(groups, group_users // TILE, ITEM_BLK // TILE)

        def group_step(operands):
            group_u, group_v, group_r, group_p, group_s = operands
            return local_pass(group_u, group_v.astype(jnp.bfloat16), group_r, group_p, group_s, TILE)
        users, partial_value, counts = lax.map(group_step, (users, block, rating, pattern, scale))
        normed = partial_value / jnp.maximum(counts, 1.0)[:, :, None] + penalty * block
        mean_square = jnp.mean(normed * normed)
        block = block - item_step * normed * lax.rsqrt(mean_square + epsilon)
        if section < SUB - 1:
            block = jnp.roll(block, 1, axis=0)
    return (users.reshape(-1, R), block.reshape(-1, R))
```

```python
import functools

import jax
import jax.numpy as jnp
from jax import lax
from jax.experimental import pallas as pl
from jax.experimental.pallas import tpu as pltpu
from jax.sharding import PartitionSpec as P

SUB = 3

penalty = 0.05
user_step = 0.01
item_step = 0.05
epsilon = 1e-06

MESH = pl.DeviceIdType.MESH
F32 = jnp.float32
BF16 = jnp.bfloat16
NT = (((1,), (1,)), ((), ()))
TN = (((0,), (0,)), ((), ()))


def wait_bytes(ref, sem):
    pltpu.make_async_copy(ref, ref, sem).wait()


def kernel(nb, nu, tile, u_hbm, v_hbm, r_hbm, pat, scl, uo_hbm, vo_hbm,
           u, rating, target, vlow, vfull, v_f32, ulow, err, cnt, cnt_in,
           psend, precv, part, nsend, nrecv, ss, ss_in, vout,
           u_sem, v_sem, r_sem, out_sem, c_send, c_recv, vl_send, vl_recv,
           vf_send, vf_recv, p_send, p_recv, fw_send, fw_recv, n_send, n_recv,
           s_send, s_recv):
    rows, rank = u.shape
    cols = rating.shape[2]
    share = v_hbm.shape[0]
    rt, ct = rows // tile, cols // tile
    g = lax.axis_index("blk")
    w = lax.axis_index("user")
    mine = pl.ds(pl.multiple_of(w * share, share), share)
    nxt = {"blk": lax.rem(g + 1, nb)}

    load_v = pltpu.make_async_copy(v_hbm, vfull.at[0, mine], v_sem)
    load_u = pltpu.make_async_copy(u_hbm, u, u_sem)
    loads = [pltpu.make_async_copy(r_hbm.at[s], rating.at[s], r_sem.at[s]) for s in range(SUB)]
    load_v.start()
    load_u.start()
    for copy in loads:
        copy.start()

    barrier = pltpu.get_barrier_semaphore()
    for d in range(1, nb):
        pl.semaphore_signal(barrier, inc=1, device_id={"blk": lax.rem(g + d, nb)}, device_id_type=MESH)
    for d in range(1, nu):
        pl.semaphore_signal(barrier, inc=1, device_id={"user": lax.rem(w + d, nu)}, device_id_type=MESH)

    for s in range(SUB):
        for j in range(ct):
            total = pat[s, 0, j]
            for a in range(1, rt):
                total = total + pat[s, a, j]
            cnt[pl.ds(s * ct + j, 1), :] = jnp.full((1, rank), (total * tile).astype(F32))
    load_v.wait()
    vlow[mine, :] = vfull[0, mine, :].astype(BF16)

    def make_target(s):
        loads[s].wait()
        for a in range(rt):
            for j in range(ct):
                block = (slice(a * tile, (a + 1) * tile), slice(j * tile, (j + 1) * tile))
                target[(s,) + block] = rating[(s,) + block].astype(F32) * scl[s, a, j]

    pl.semaphore_wait(barrier, nb - 1 + nu - 1)

    sends = []

    def send(src, dst, one, two, where):
        copy = pltpu.make_async_remote_copy(
            src_ref=src, dst_ref=dst, send_sem=one, recv_sem=two, device_id=where, device_id_type=MESH
        )
        copy.start()
        return copy

    others = [{"user": lax.rem(w + d, nu)} for d in range(1, nu)]
    first = []
    for d, where in enumerate(others):
        first.append(send(vlow.at[mine], vlow.at[mine], vl_send.at[d], vl_recv.at[d], where))
    for d, where in enumerate(others):
        first.append(send(vfull.at[0, mine], vfull.at[0, mine], vf_send.at[d], vf_recv.at[d], where))
        first.append(send(cnt, cnt_in.at[d], c_send.at[d], c_recv.at[d], where))

    make_target(0)
    load_u.wait()

    for s in range(SUB):
        last = s == SUB - 1
        if s == 0:
            for copy in first[: nu - 1]:
                copy.wait_recv()
        v_low = vlow[...]

        def errors(low, a):
            predicted = lax.dot_general(low, v_low, NT, preferred_element_type=F32)
            out = []
            for j in range(ct):
                columns = slice(j * tile, (j + 1) * tile)
                diff = predicted[:, columns] - target[s, a * tile:(a + 1) * tile, columns]
                out.append((pat[s, a, j].astype(F32) * diff).astype(BF16))
            return jnp.concatenate(out, axis=1)

        for a in range(rt):
            span = slice(a * tile, (a + 1) * tile)
            old = u[span, :]
            one = errors(old.astype(BF16), a)
            grad = jnp.dot(one, v_low, preferred_element_type=F32) + penalty * old
            new = old - user_step * grad
            u[span, :] = new
            low = new.astype(BF16)
            ulow[span, :] = low
            err[span, :] = errors(low, a)

        exchanged = []
        for j in range(ct):
            columns = slice(j * tile, (j + 1) * tile)
            value = lax.dot_general(err[:, columns], ulow[...], TN, preferred_element_type=F32)
            part[columns, :] = value
            psend[s, columns, :] = value.astype(BF16)
            for d, where in enumerate(others):
                exchanged.append(send(
                    psend.at[s, columns], precv.at[s, d, columns], p_send.at[s, d, j], p_recv.at[s, d, j], where
                ))

        if last:
            store_u = pltpu.make_async_copy(u, uo_hbm, u_sem)
            store_u.start()
        if s == 0:
            for copy in first[nu - 1:]:
                copy.wait_recv()
            for copy in first:
                copy.wait_send()
            total = cnt[...]
            for d in range(nu - 1):
                total = total + cnt_in[d]
            cnt[...] = 1.0 / jnp.maximum(total, 1.0)
        if not last:
            forward = send(vfull.at[s], vfull.at[s + 1], fw_send.at[s], fw_recv.at[s], nxt)
            make_target(s + 1)

        squares = jnp.zeros((8, rank), F32)
        for j in range(ct):
            columns = slice(j * tile, (j + 1) * tile)
            for d in range(nu - 1):
                exchanged[j * (nu - 1) + d].wait()
            total = part[columns, :]
            for d in range(nu - 1):
                total = total + precv[s, d, columns, :].astype(F32)
            v_old = vfull[s, columns, :] if s == 0 else v_f32[columns, :]
            normed = total * cnt[pl.ds(s * ct + j, 1), :] + penalty * v_old
            squares = squares + jnp.sum((normed * normed).reshape(tile // 8, 8, rank), axis=0)
            if last:
                part[columns, :] = normed
            else:
                nsend[s, columns, :] = normed.astype(BF16)
        ss[s] = jnp.sum(squares, axis=0, keepdims=True)
        for d in range(1, nb):
            send(ss.at[s], ss_in.at[s, d - 1], s_send.at[s], s_recv.at[s], {"blk": lax.rem(g + d, nb)})
        if not last:
            ahead = send(nsend.at[s], nrecv.at[s], n_send.at[s], n_recv.at[s], nxt)

        wait_bytes(ss_in.at[s], s_recv.at[s])
        total = ss[s] + jnp.sum(ss_in[s], axis=0)
        mean = jnp.sum(total, axis=1, keepdims=True) / (nb * cols * rank)
        gain = item_step * lax.rsqrt(mean + epsilon)
        if not last:
            forward.wait()
            ahead.wait()
            fresh = vfull[s + 1] - gain * nrecv[s].astype(F32)
            v_f32[...] = fresh
            vlow[...] = fresh.astype(BF16)
            if s + 1 < SUB - 1:
                vfull[s + 1] = fresh
        else:
            vout[...] = v_f32[mine, :] - gain * part[mine, :]
            store_v = pltpu.make_async_copy(vout, vo_hbm, v_sem)
            store_v.start()
    for s in range(SUB):
        wait_bytes(ss_in.at[s], s_send.at[s])
    store_u.wait()
    store_v.wait()


def shards(user_factors, item_factors, ratings, tile_pattern, tile_scale):
    nb, nu = lax.axis_size("blk"), lax.axis_size("user")
    tile = ratings.shape[2] // tile_pattern.shape[2]
    rows, rank = user_factors.shape
    share = item_factors.shape[0]
    cols = ratings.shape[2]
    ct = cols // tile
    counts = -(-SUB * ct // 8) * 8
    dma = pltpu.SemaphoreType.DMA
    vmem = pltpu.VMEM
    hbm = pl.BlockSpec(memory_space=pl.ANY)
    smem = pl.BlockSpec(memory_space=pltpu.SMEM)
    return pl.pallas_call(
        functools.partial(kernel, nb, nu, tile),
        out_shape=(
            jax.ShapeDtypeStruct(user_factors.shape, F32),
            jax.ShapeDtypeStruct(item_factors.shape, F32),
        ),
        in_specs=[hbm, hbm, hbm, smem, smem],
        out_specs=(hbm, hbm),
        scratch_shapes=[
            vmem((rows, rank), F32),
            vmem((SUB, rows, cols), BF16),
            vmem((SUB, rows, cols), F32),
            vmem((cols, rank), BF16),
            vmem((SUB, cols, rank), F32),
            vmem((cols, rank), F32),
            vmem((rows, rank), BF16),
            vmem((rows, cols), BF16),
            vmem((counts, rank), F32),
            vmem((nu - 1, counts, rank), F32),
            vmem((SUB, cols, rank), BF16),
            vmem((SUB, nu - 1, cols, rank), BF16),
            vmem((cols, rank), F32),
            vmem((SUB - 1, cols, rank), BF16),
            vmem((SUB - 1, cols, rank), BF16),
            vmem((SUB, 1, rank), F32),
            vmem((SUB, nb - 1, 1, rank), F32),
            vmem((share, rank), F32),
            dma(()), dma(()), dma((SUB,)), dma(()),
            dma((nu - 1,)), dma((nu - 1,)),
            dma((nu - 1,)), dma((nu - 1,)),
            dma((nu - 1,)), dma((nu - 1,)),
            dma((SUB, nu - 1, ct)), dma((SUB, nu - 1, ct)),
            dma((SUB - 1,)), dma((SUB - 1,)),
            dma((SUB - 1,)), dma((SUB - 1,)),
            dma((SUB,)), dma((SUB,)),
        ],
        compiler_params=pltpu.CompilerParams(collective_id=0, has_side_effects=True),
    )(user_factors, item_factors, ratings, tile_pattern, tile_scale)


def solution(mesh):
    specs = (
        P(("blk", "user"), None),
        P(("blk", "user"), None),
        P(None, ("blk", "user"), None),
        P(None, ("blk", "user"), None),
        P(None, ("blk", "user"), None),
    )
    out_specs = (P(("blk", "user"), None), P(("blk", "user"), None))
    return jax.shard_map(shards, mesh=mesh, in_specs=specs, out_specs=out_specs, check_vma=False)
```

```python
import functools

import jax
import jax.numpy as jnp
from jax import lax
from jax.experimental import pallas as pl
from jax.experimental.pallas import tpu as pltpu
from jax.sharding import PartitionSpec as P

SUB = 3
SIDES = (1, 2)
LAYER = 4

penalty = 0.05
user_step = 0.01
item_step = 0.05
epsilon = 1e-06

MESH = pl.DeviceIdType.MESH
F32 = jnp.float32
BF16 = jnp.bfloat16
NT = (((1,), (1,)), ((), ()))
TN = (((0,), (0,)), ((), ()))


def wait_bytes(ref, sem):
    pltpu.make_async_copy(ref, ref, sem).wait()


def kernel(nb, nu, tile, u_hbm, v_hbm, r_hbm, pat, scl, u, vout,
           rating, target, vlow, vfull, v_f32, ulow, err, cnt, cnt_in,
           psend, precv, part, nsend, nrecv, ss, ss_in,
           u_sem, v_sem, r_sem, c_send, c_recv, vl_send, vl_recv,
           vf_send, vf_recv, p_send, p_recv, fw_send, fw_recv, n_send, n_recv,
           s_send, s_recv, up_sem, down_sem, side_sem):
    rows, rank = u.shape
    cols = rating.shape[2]
    share = v_hbm.shape[0]
    rt, ct = rows // tile, cols // tile
    g = lax.axis_index("blk")
    w = lax.axis_index("user")
    mine = pl.ds(pl.multiple_of(w * share, share), share)
    nxt = {"blk": lax.rem(g + 1, nb)}

    load_v = pltpu.make_async_copy(v_hbm, vfull.at[0, mine], v_sem)
    load_u = pltpu.make_async_copy(u_hbm, u, u_sem)
    loads = [pltpu.make_async_copy(r_hbm.at[s], rating.at[s], r_sem.at[s]) for s in range(SUB)]
    load_v.start()
    load_u.start()
    for copy in loads:
        copy.start()

    barrier = pltpu.get_barrier_semaphore()
    def signal(sem, where):
        pl.semaphore_signal(sem, inc=1, device_id=where, device_id_type=MESH)

    layers = nb // LAYER
    z = lax.div(g, LAYER)
    below, above = z > 0, z < layers - 1
    lower = {"blk": lax.rem(g + nb - LAYER, nb)}
    upper = {"blk": lax.rem(g + LAYER, nb)}
    beside = [{"blk": g + d - 2 * d * lax.rem(lax.div(g, d), 2)} for d in SIDES]
    for d in range(1, nu):
        signal(barrier, {"user": lax.rem(w + d, nu)})
    for where in beside:
        signal(barrier, where)
    pl.when(below)(lambda: signal(barrier, lower))
    pl.when(above)(lambda: signal(barrier, upper))
    greeted = nu - 1 + len(SIDES) + below.astype(jnp.int32) + above.astype(jnp.int32)

    def upward():
        pl.when(below)(lambda: pl.semaphore_wait(up_sem, 1))
        pl.when(above)(lambda: signal(up_sem, upper))

    def downward():
        pl.when(above)(lambda: pl.semaphore_wait(down_sem, 1))
        pl.when(below)(lambda: signal(down_sem, lower))

    for s in range(SUB):
        for j in range(ct):
            total = pat[s, j, 0]
            for a in range(1, rt):
                total = total + pat[s, j, a]
            cnt[pl.ds(s * ct + j, 1), :] = jnp.full((1, rank), (total * tile).astype(F32))
    load_v.wait()
    vlow[mine, :] = vfull[0, mine, :].astype(BF16)

    def make_target(s):
        loads[s].wait()
        for a in range(rt):
            for j in range(ct):
                block = (slice(a * tile, (a + 1) * tile), slice(j * tile, (j + 1) * tile))
                target[(s,) + block] = rating[(s,) + block].astype(F32) * scl[s, j, a]

    pl.semaphore_wait(barrier, greeted)

    sends = []

    def send(src, dst, one, two, where):
        copy = pltpu.make_async_remote_copy(
            src_ref=src, dst_ref=dst, send_sem=one, recv_sem=two, device_id=where, device_id_type=MESH
        )
        copy.start()
        return copy

    others = [{"user": lax.rem(w + d, nu)} for d in range(1, nu)]
    first = []
    for d, where in enumerate(others):
        first.append(send(vlow.at[mine], vlow.at[mine], vl_send.at[d], vl_recv.at[d], where))
    for d, where in enumerate(others):
        first.append(send(vfull.at[0, mine], vfull.at[0, mine], vf_send.at[d], vf_recv.at[d], where))
        first.append(send(cnt, cnt_in.at[d], c_send.at[d], c_recv.at[d], where))

    @pl.when(2 * z < layers)
    def _():
        upward()
        downward()

    @pl.when(2 * z >= layers)
    def _():
        downward()
        upward()

    signal(side_sem.at[0], beside[0])
    make_target(0)
    load_u.wait()

    for s in range(SUB):
        last = s == SUB - 1
        if s == 0:
            for copy in first[: nu - 1]:
                copy.wait_recv()
            for k in range(1, len(SIDES)):
                pl.semaphore_wait(side_sem.at[k - 1], 1)
                signal(side_sem.at[k], beside[k])
        v_low = vlow[...]

        def errors(low, a):
            predicted = lax.dot_general(low, v_low, NT, preferred_element_type=F32)
            out = []
            for j in range(ct):
                columns = slice(j * tile, (j + 1) * tile)
                diff = predicted[:, columns] - target[s, a * tile:(a + 1) * tile, columns]
                out.append((pat[s, j, a].astype(F32) * diff).astype(BF16))
            return jnp.concatenate(out, axis=1)

        for a in range(rt):
            span = slice(a * tile, (a + 1) * tile)
            old = u[span, :]
            one = errors(old.astype(BF16), a)
            grad = jnp.dot(one, v_low, preferred_element_type=F32) + penalty * old
            new = old - user_step * grad
            u[span, :] = new
            low = new.astype(BF16)
            ulow[span, :] = low
            err[span, :] = errors(low, a)

        exchanged = []
        for j in range(ct):
            columns = slice(j * tile, (j + 1) * tile)
            value = lax.dot_general(err[:, columns], ulow[...], TN, preferred_element_type=F32)
            part[columns, :] = value
            psend[s, columns, :] = value.astype(BF16)
            for d, where in enumerate(others):
                exchanged.append(send(
                    psend.at[s, columns], precv.at[s, d, columns], p_send.at[s, d, j], p_recv.at[s, d, j], where
                ))

        if s == 0:
            pl.semaphore_wait(side_sem.at[len(SIDES) - 1], 1)
            for copy in first[nu - 1:]:
                copy.wait_recv()
            for copy in first:
                copy.wait_send()
            total = cnt[...]
            for d in range(nu - 1):
                total = total + cnt_in[d]
            cnt[...] = 1.0 / jnp.maximum(total, 1.0)
        if not last:
            forward = send(vfull.at[s], vfull.at[s + 1], fw_send.at[s], fw_recv.at[s], nxt)
            make_target(s + 1)

        squares = jnp.zeros((8, rank), F32)
        for j in range(ct):
            columns = slice(j * tile, (j + 1) * tile)
            for d in range(nu - 1):
                exchanged[j * (nu - 1) + d].wait()
            total = part[columns, :]
            for d in range(nu - 1):
                total = total + precv[s, d, columns, :].astype(F32)
            v_old = vfull[s, columns, :] if s == 0 else v_f32[columns, :]
            normed = total * cnt[pl.ds(s * ct + j, 1), :] + penalty * v_old
            squares = squares + jnp.sum((normed * normed).reshape(tile // 8, 8, rank), axis=0)
            if last:
                part[columns, :] = normed
            else:
                nsend[s, columns, :] = normed
        ss[s] = jnp.sum(squares, axis=0, keepdims=True)
        for d in range(1, nb):
            send(ss.at[s], ss_in.at[s, d - 1], s_send.at[s], s_recv.at[s], {"blk": lax.rem(g + d, nb)})
        if not last:
            ahead = send(nsend.at[s], nrecv.at[s], n_send.at[s], n_recv.at[s], nxt)

        wait_bytes(ss_in.at[s], s_recv.at[s])
        total = ss[s] + jnp.sum(ss_in[s], axis=0)
        mean = jnp.sum(total, axis=1, keepdims=True) / (nb * cols * rank)
        gain = item_step * lax.rsqrt(mean + epsilon)
        if not last:
            forward.wait()
            ahead.wait()
            fresh = vfull[s + 1] - gain * nrecv[s].astype(F32)
            v_f32[...] = fresh
            vlow[...] = fresh.astype(BF16)
            if s + 1 < SUB - 1:
                vfull[s + 1] = fresh
        else:
            vout[...] = v_f32[mine, :] - gain * part[mine, :]
    for s in range(SUB):
        wait_bytes(ss_in.at[s], s_send.at[s])


def hand_over(u, v, uo_hbm, vo_hbm, sem):
    copies = [pltpu.make_async_copy(v, vo_hbm, sem.at[0]), pltpu.make_async_copy(u, uo_hbm, sem.at[1])]
    for copy in copies:
        copy.start()
    for copy in copies:
        copy.wait()


def shards(user_factors, item_factors, ratings, tile_pattern, tile_scale):
    nb, nu = lax.axis_size("blk"), lax.axis_size("user")
    tile = ratings.shape[2] // tile_pattern.shape[2]
    rows, rank = user_factors.shape
    share = item_factors.shape[0]
    cols = ratings.shape[2]
    ct = cols // tile
    counts = -(-SUB * ct // 8) * 8
    dma = pltpu.SemaphoreType.DMA
    vmem = pltpu.VMEM
    hbm = pl.BlockSpec(memory_space=pl.ANY)
    whole = pl.BlockSpec(memory_space=pltpu.VMEM)
    smem = pl.BlockSpec(memory_space=pltpu.SMEM)
    users, items = pl.pallas_call(
        functools.partial(kernel, nb, nu, tile),
        out_shape=(vmem(user_factors.shape, F32), vmem(item_factors.shape, F32)),
        in_specs=[hbm, hbm, hbm, smem, smem],
        out_specs=(whole, whole),
        scratch_shapes=[
            vmem((SUB, rows, cols), BF16),
            vmem((SUB, rows, cols), F32),
            vmem((cols, rank), BF16),
            vmem((SUB, cols, rank), F32),
            vmem((cols, rank), F32),
            vmem((rows, rank), BF16),
            vmem((rows, cols), BF16),
            vmem((counts, rank), F32),
            vmem((nu - 1, counts, rank), F32),
            vmem((SUB, cols, rank), BF16),
            vmem((SUB, nu - 1, cols, rank), BF16),
            vmem((cols, rank), F32),
            vmem((SUB - 1, cols, rank), F32),
            vmem((SUB - 1, cols, rank), F32),
            vmem((SUB, 1, rank), F32),
            vmem((SUB, nb - 1, 1, rank), F32),
            dma(()), dma(()), dma((SUB,)),
            dma((nu - 1,)), dma((nu - 1,)),
            dma((nu - 1,)), dma((nu - 1,)),
            dma((nu - 1,)), dma((nu - 1,)),
            dma((SUB, nu - 1, ct)), dma((SUB, nu - 1, ct)),
            dma((SUB - 1,)), dma((SUB - 1,)),
            dma((SUB - 1,)), dma((SUB - 1,)),
            dma((SUB,)), dma((SUB,)),
            pltpu.SemaphoreType.REGULAR, pltpu.SemaphoreType.REGULAR,
            pltpu.SemaphoreType.REGULAR((len(SIDES),)),
        ],
        compiler_params=pltpu.CompilerParams(collective_id=0, has_side_effects=True),
    )(user_factors, item_factors, ratings, jnp.swapaxes(tile_pattern, 1, 2), jnp.swapaxes(tile_scale, 1, 2))
    return pl.pallas_call(
        hand_over,
        out_shape=(
            jax.ShapeDtypeStruct(user_factors.shape, F32),
            jax.ShapeDtypeStruct(item_factors.shape, F32),
        ),
        in_specs=[whole, whole],
        out_specs=(hbm, hbm),
        scratch_shapes=[dma((2,))],
    )(pltpu.with_memory_space_constraint(users, pltpu.VMEM), pltpu.with_memory_space_constraint(items, pltpu.VMEM))


def solution(mesh):
    specs = (
        P(("blk", "user"), None),
        P(("blk", "user"), None),
        P(None, ("blk", "user"), None),
        P(None, ("blk", "user"), None),
        P(None, ("blk", "user"), None),
    )
    out_specs = (P(("blk", "user"), None), P(("blk", "user"), None))
    return jax.shard_map(shards, mesh=mesh, in_specs=specs, out_specs=out_specs, check_vma=False)
```

```python
import functools

import jax
import jax.numpy as jnp
from jax import lax
from jax.experimental import pallas as pl
from jax.experimental.pallas import tpu as pltpu
from jax.sharding import PartitionSpec as P

SUB = 3
SIDES = (1, 2)
LAYER = 4

penalty = 0.05
user_step = 0.01
item_step = 0.05
epsilon = 1e-06

MESH = pl.DeviceIdType.MESH
F32 = jnp.float32
BF16 = jnp.bfloat16
NT = (((1,), (1,)), ((), ()))
TN = (((0,), (0,)), ((), ()))


def wait_bytes(ref, sem):
    pltpu.make_async_copy(ref, ref, sem).wait()


def kernel(nb, nu, tile, u_hbm, v_hbm, r_hbm, pat, scl, u, vout,
           rating, target, vlow, vfull, v_f32, ulow, err, cnt, cnt_in,
           psend, precv, part, nsend, nrecv, ss, ss_in,
           u_sem, v_sem, r_sem, c_send, c_recv, vl_send, vl_recv,
           vf_send, vf_recv, p_send, p_recv, fw_send, fw_recv, n_send, n_recv,
           s_send, s_recv, up_sem, down_sem, side_sem,
           rating_p, target_p, u_p, meta, meta_in, m_send, m_recv):
    rows, rank = u.shape
    cols = rating.shape[2]
    share = v_hbm.shape[0]
    rt, ct = rows // tile, cols // tile
    g = lax.axis_index("blk")
    w = lax.axis_index("user")
    mine = pl.ds(pl.multiple_of(w * share, share), share)
    nxt = {"blk": lax.rem(g + 1, nb)}

    load_v = pltpu.make_async_copy(v_hbm, vfull.at[0, mine], v_sem)
    load_u = pltpu.make_async_copy(u_hbm, u, u_sem)
    loads = [pltpu.make_async_copy(r_hbm.at[s], rating.at[s], r_sem.at[s]) for s in range(SUB)]
    load_v.start()
    load_u.start()
    for copy in loads:
        copy.start()

    barrier = pltpu.get_barrier_semaphore()
    def signal(sem, where):
        pl.semaphore_signal(sem, inc=1, device_id=where, device_id_type=MESH)

    layers = nb // LAYER
    z = lax.div(g, LAYER)
    below, above = z > 0, z < layers - 1
    lower = {"blk": lax.rem(g + nb - LAYER, nb)}
    upper = {"blk": lax.rem(g + LAYER, nb)}
    beside = [{"blk": g + d - 2 * d * lax.rem(lax.div(g, d), 2)} for d in SIDES]
    for d in range(1, nu):
        signal(barrier, {"user": lax.rem(w + d, nu)})
    for where in beside:
        signal(barrier, where)
    pl.when(below)(lambda: signal(barrier, lower))
    pl.when(above)(lambda: signal(barrier, upper))
    greeted = nu - 1 + len(SIDES) + below.astype(jnp.int32) + above.astype(jnp.int32)

    def upward():
        pl.when(below)(lambda: pl.semaphore_wait(up_sem, 1))
        pl.when(above)(lambda: signal(up_sem, upper))

    def downward():
        pl.when(above)(lambda: pl.semaphore_wait(down_sem, 1))
        pl.when(below)(lambda: signal(down_sem, lower))

    for s in range(SUB):
        for j in range(ct):
            total = pat[s, j, 0]
            for a in range(1, rt):
                total = total + pat[s, j, a]
            cnt[pl.ds(s * ct + j, 1), :] = jnp.full((1, rank), (total * tile).astype(F32))
    mirrored = nu == 2

    def meta_row(kind, a, j):
        return pl.ds((kind * rt + a) * ct + j, 1)

    if mirrored:
        for a in range(rt):
            for j in range(ct):
                meta[meta_row(0, a, j), :] = jnp.full((1, tile), pat[SUB - 1, j, a].astype(F32))
                meta[meta_row(1, a, j), :] = jnp.full((1, tile), scl[SUB - 1, j, a])
    load_v.wait()
    vlow[mine, :] = vfull[0, mine, :].astype(BF16)

    def make_target(s):
        loads[s].wait()
        for a in range(rt):
            for j in range(ct):
                block = (slice(a * tile, (a + 1) * tile), slice(j * tile, (j + 1) * tile))
                target[(s,) + block] = rating[(s,) + block].astype(F32) * scl[s, j, a]

    pl.semaphore_wait(barrier, greeted)

    sends = []

    def send(src, dst, one, two, where):
        copy = pltpu.make_async_remote_copy(
            src_ref=src, dst_ref=dst, send_sem=one, recv_sem=two, device_id=where, device_id_type=MESH
        )
        copy.start()
        return copy

    others = [{"user": lax.rem(w + d, nu)} for d in range(1, nu)]
    first = []
    for d, where in enumerate(others):
        first.append(send(vlow.at[mine], vlow.at[mine], vl_send.at[d], vl_recv.at[d], where))
    for d, where in enumerate(others):
        first.append(send(vfull.at[0, mine], vfull.at[0, mine], vf_send.at[d], vf_recv.at[d], where))
        first.append(send(cnt, cnt_in.at[d], c_send.at[d], c_recv.at[d], where))

    if mirrored:
        meta_ahead = send(meta, meta_in, m_send.at[2], m_recv.at[2], others[0])

    @pl.when(2 * z < layers)
    def _():
        upward()
        downward()

    @pl.when(2 * z >= layers)
    def _():
        downward()
        upward()

    signal(side_sem.at[0], beside[0])
    make_target(0)
    load_u.wait()

    for s in range(SUB):
        last = s == SUB - 1
        if s == 0:
            for copy in first[: nu - 1]:
                copy.wait_recv()
            for k in range(1, len(SIDES)):
                pl.semaphore_wait(side_sem.at[k - 1], 1)
                signal(side_sem.at[k], beside[k])
        v_low = vlow[...]

        both = mirrored and last
        if both:
            users_ahead.wait()

        def own_tile(a, j):
            return (
                pat[s, j, a].astype(F32),
                target[s, a * tile:(a + 1) * tile, j * tile:(j + 1) * tile],
            )

        def partner_tile(a, j):
            return (
                meta_in[meta_row(0, a, j), :],
                target_p[a * tile:(a + 1) * tile, j * tile:(j + 1) * tile],
            )

        def errors(low, a, tile_of):
            predicted = lax.dot_general(low, v_low, NT, preferred_element_type=F32)
            out = []
            for j in range(ct):
                weight, goal = tile_of(a, j)
                diff = predicted[:, j * tile:(j + 1) * tile] - goal
                out.append((weight * diff).astype(BF16))
            return jnp.concatenate(out, axis=1)

        sets = [(u, 0, own_tile)] + ([(u_p, rows, partner_tile)] if both else [])
        for a in range(rt):
            for held, start, tile_of in sets:
                span = slice(a * tile, (a + 1) * tile)
                place = slice(start + a * tile, start + (a + 1) * tile)
                old = held[span, :].astype(F32)
                one = errors(old.astype(BF16), a, tile_of)
                grad = jnp.dot(one, v_low, preferred_element_type=F32) + penalty * old
                new = old - user_step * grad
                if held is u:
                    u[span, :] = new
                low = new.astype(BF16)
                ulow[place, :] = low
                err[place, :] = errors(low, a, tile_of)

        exchanged = []
        for j in range(ct):
            columns = slice(j * tile, (j + 1) * tile)
            deep = slice(0, len(sets) * rows)
            value = lax.dot_general(err[deep, columns], ulow[deep, :], TN, preferred_element_type=F32)
            part[columns, :] = value
            if both:
                continue
            psend[s, columns, :] = value.astype(BF16)
            for d, where in enumerate(others):
                exchanged.append(send(
                    psend.at[s, columns], precv.at[s, d, columns], p_send.at[s, d, j], p_recv.at[s, d, j], where
                ))

        if s == 0:
            pl.semaphore_wait(side_sem.at[len(SIDES) - 1], 1)
            for copy in first[nu - 1:]:
                copy.wait_recv()
            for copy in first:
                copy.wait_send()
            total = cnt[...]
            for d in range(nu - 1):
                total = total + cnt_in[d]
            cnt[...] = 1.0 / jnp.maximum(total, 1.0)
        if not last:
            forward = send(vfull.at[s], vfull.at[s + 1], fw_send.at[s], fw_recv.at[s], nxt)
            make_target(s + 1)
        if mirrored and s == SUB - 2:
            ratings_ahead.wait()
            meta_ahead.wait()
            for a in range(rt):
                for j in range(ct):
                    block = (slice(a * tile, (a + 1) * tile), slice(j * tile, (j + 1) * tile))
                    target_p[block] = rating_p[block].astype(F32) * meta_in[meta_row(1, a, j), :]

        squares = jnp.zeros((8, rank), F32)
        for j in range(ct):
            columns = slice(j * tile, (j + 1) * tile)
            for d in range(0 if both else nu - 1):
                exchanged[j * (nu - 1) + d].wait()
            total = part[columns, :]
            for d in range(0 if both else nu - 1):
                total = total + precv[s, d, columns, :].astype(F32)
            v_old = vfull[s, columns, :] if s == 0 else v_f32[columns, :]
            normed = total * cnt[pl.ds(s * ct + j, 1), :] + penalty * v_old
            squares = squares + jnp.sum((normed * normed).reshape(tile // 8, 8, rank), axis=0)
            if last:
                part[columns, :] = normed
            else:
                nsend[s, columns, :] = normed
        ss[s] = jnp.sum(squares, axis=0, keepdims=True)
        for d in range(1, nb):
            send(ss.at[s], ss_in.at[s, d - 1], s_send.at[s], s_recv.at[s], {"blk": lax.rem(g + d, nb)})
        if not last:
            ahead = send(nsend.at[s], nrecv.at[s], n_send.at[s], n_recv.at[s], nxt)

        if mirrored and s == 0:
            ratings_ahead = send(r_hbm.at[SUB - 1], rating_p, m_send.at[0], m_recv.at[0], others[0])
        if mirrored and s == SUB - 2:
            users_ahead = send(ulow.at[pl.ds(0, rows)], u_p, m_send.at[1], m_recv.at[1], others[0])
        wait_bytes(ss_in.at[s], s_recv.at[s])
        total = ss[s] + jnp.sum(ss_in[s], axis=0)
        mean = jnp.sum(total, axis=1, keepdims=True) / (nb * cols * rank)
        gain = item_step * lax.rsqrt(mean + epsilon)
        if not last:
            forward.wait()
            ahead.wait()
            fresh = vfull[s + 1] - gain * nrecv[s].astype(F32)
            v_f32[...] = fresh
            vlow[...] = fresh.astype(BF16)
            if s + 1 < SUB - 1:
                vfull[s + 1] = fresh
        else:
            vout[...] = v_f32[mine, :] - gain * part[mine, :]
    for s in range(SUB):
        wait_bytes(ss_in.at[s], s_send.at[s])


def hand_over(u, v, uo_hbm, vo_hbm, sem):
    copies = [pltpu.make_async_copy(v, vo_hbm, sem.at[0]), pltpu.make_async_copy(u, uo_hbm, sem.at[1])]
    for copy in copies:
        copy.start()
    for copy in copies:
        copy.wait()


def shards(user_factors, item_factors, ratings, tile_pattern, tile_scale):
    nb, nu = lax.axis_size("blk"), lax.axis_size("user")
    tile = ratings.shape[2] // tile_pattern.shape[2]
    rows, rank = user_factors.shape
    share = item_factors.shape[0]
    cols = ratings.shape[2]
    ct = cols // tile
    counts = -(-SUB * ct // 8) * 8
    marks = -(-2 * (rows // tile) * ct // 8) * 8
    dma = pltpu.SemaphoreType.DMA
    vmem = pltpu.VMEM
    hbm = pl.BlockSpec(memory_space=pl.ANY)
    whole = pl.BlockSpec(memory_space=pltpu.VMEM)
    smem = pl.BlockSpec(memory_space=pltpu.SMEM)
    users, items = pl.pallas_call(
        functools.partial(kernel, nb, nu, tile),
        out_shape=(vmem(user_factors.shape, F32), vmem(item_factors.shape, F32)),
        in_specs=[hbm, hbm, hbm, smem, smem],
        out_specs=(whole, whole),
        scratch_shapes=[
            vmem((SUB, rows, cols), BF16),
            vmem((SUB, rows, cols), F32),
            vmem((cols, rank), BF16),
            vmem((SUB, cols, rank), F32),
            vmem((cols, rank), F32),
            vmem((2 * rows, rank), BF16),
            vmem((2 * rows, cols), BF16),
            vmem((counts, rank), F32),
            vmem((nu - 1, counts, rank), F32),
            vmem((SUB, cols, rank), BF16),
            vmem((SUB, nu - 1, cols, rank), BF16),
            vmem((cols, rank), F32),
            vmem((SUB - 1, cols, rank), F32),
            vmem((SUB - 1, cols, rank), F32),
            vmem((SUB, 1, rank), F32),
            vmem((SUB, nb - 1, 1, rank), F32),
            dma(()), dma(()), dma((SUB,)),
            dma((nu - 1,)), dma((nu - 1,)),
            dma((nu - 1,)), dma((nu - 1,)),
            dma((nu - 1,)), dma((nu - 1,)),
            dma((SUB, nu - 1, ct)), dma((SUB, nu - 1, ct)),
            dma((SUB - 1,)), dma((SUB - 1,)),
            dma((SUB - 1,)), dma((SUB - 1,)),
            dma((SUB,)), dma((SUB,)),
            pltpu.SemaphoreType.REGULAR, pltpu.SemaphoreType.REGULAR,
            pltpu.SemaphoreType.REGULAR((len(SIDES),)),
            vmem((rows, cols), BF16),
            vmem((rows, cols), F32),
            vmem((rows, rank), BF16),
            vmem((marks, tile), F32),
            vmem((marks, tile), F32),
            dma((3,)), dma((3,)),
        ],
        compiler_params=pltpu.CompilerParams(collective_id=0, has_side_effects=True),
    )(user_factors, item_factors, ratings, jnp.swapaxes(tile_pattern, 1, 2), jnp.swapaxes(tile_scale, 1, 2))
    return pl.pallas_call(
        hand_over,
        out_shape=(
            jax.ShapeDtypeStruct(user_factors.shape, F32),
            jax.ShapeDtypeStruct(item_factors.shape, F32),
        ),
        in_specs=[whole, whole],
        out_specs=(hbm, hbm),
        scratch_shapes=[dma((2,))],
    )(pltpu.with_memory_space_constraint(users, pltpu.VMEM), pltpu.with_memory_space_constraint(items, pltpu.VMEM))


def solution(mesh):
    specs = (
        P(("blk", "user"), None),
        P(("blk", "user"), None),
        P(None, ("blk", "user"), None),
        P(None, ("blk", "user"), None),
        P(None, ("blk", "user"), None),
    )
    out_specs = (P(("blk", "user"), None), P(("blk", "user"), None))
    return jax.shard_map(shards, mesh=mesh, in_specs=specs, out_specs=out_specs, check_vma=False)
```

```python
import functools

import jax
import jax.numpy as jnp
from jax import lax
from jax.experimental import pallas as pl
from jax.experimental.pallas import tpu as pltpu
from jax.sharding import PartitionSpec as P

SUB = 3
SIDES = (1, 2)
LAYER = 4

penalty = 0.05
user_step = 0.01
item_step = 0.05
epsilon = 1e-06

MESH = pl.DeviceIdType.MESH
F32 = jnp.float32
BF16 = jnp.bfloat16
NT = (((1,), (1,)), ((), ()))
TN = (((0,), (0,)), ((), ()))


def wait_bytes(ref, sem):
    pltpu.make_async_copy(ref, ref, sem).wait()


def kernel(nb, nu, tile, u_hbm, v_hbm, r_hbm, pat, scl, u, vout,
           rating, target, vlow, vfull, v_f32, ulow, err, cnt, cnt_in,
           psend, precv, part, nsend, nrecv, ss, ss_in,
           u_sem, v_sem, r_sem, c_send, c_recv, vl_send, vl_recv,
           vf_send, vf_recv, p_send, p_recv, fw_send, fw_recv, n_send, n_recv,
           s_send, s_recv, up_sem, down_sem, side_sem,
           rating_p, target_p, u_p, meta, meta_in, m_send, m_recv):
    rows, rank = u.shape
    cols = rating.shape[2]
    share = v_hbm.shape[0]
    rt, ct = rows // tile, cols // tile
    g = lax.axis_index("blk")
    w = lax.axis_index("user")
    mine = pl.ds(pl.multiple_of(w * share, share), share)
    nxt = {"blk": lax.rem(g + 1, nb)}

    load_v = pltpu.make_async_copy(v_hbm, vfull.at[0, mine], v_sem)
    load_u = pltpu.make_async_copy(u_hbm, u, u_sem)
    loads = [pltpu.make_async_copy(r_hbm.at[s], rating.at[s], r_sem.at[s]) for s in range(SUB)]
    load_v.start()
    load_u.start()
    for copy in loads:
        copy.start()

    barrier = pltpu.get_barrier_semaphore()
    def signal(sem, where):
        pl.semaphore_signal(sem, inc=1, device_id=where, device_id_type=MESH)

    layers = nb // LAYER
    z = lax.div(g, LAYER)
    below, above = z > 0, z < layers - 1
    lower = {"blk": lax.rem(g + nb - LAYER, nb)}
    upper = {"blk": lax.rem(g + LAYER, nb)}
    beside = [{"blk": g + d - 2 * d * lax.rem(lax.div(g, d), 2)} for d in SIDES]
    for d in range(1, nu):
        signal(barrier, {"user": lax.rem(w + d, nu)})
    for where in beside:
        signal(barrier, where)
    pl.when(below)(lambda: signal(barrier, lower))
    pl.when(above)(lambda: signal(barrier, upper))
    greeted = nu - 1 + len(SIDES) + below.astype(jnp.int32) + above.astype(jnp.int32)

    def upward():
        pl.when(below)(lambda: pl.semaphore_wait(up_sem, 1))
        pl.when(above)(lambda: signal(up_sem, upper))

    def downward():
        pl.when(above)(lambda: pl.semaphore_wait(down_sem, 1))
        pl.when(below)(lambda: signal(down_sem, lower))

    for s in range(SUB):
        for j in range(ct):
            total = pat[s, j, 0]
            for a in range(1, rt):
                total = total + pat[s, j, a]
            cnt[pl.ds(s * ct + j, 1), :] = jnp.full((1, rank), (total * tile).astype(F32))
    mirrored = nu == 2

    def meta_row(kind, a, j):
        return pl.ds((kind * rt + a) * ct + j, 1)

    if mirrored:
        for a in range(rt):
            for j in range(ct):
                meta[meta_row(0, a, j), :] = jnp.full((1, tile), pat[SUB - 1, j, a].astype(F32))
                meta[meta_row(1, a, j), :] = jnp.full((1, tile), scl[SUB - 1, j, a])
    load_v.wait()
    vlow[mine, :] = vfull[0, mine, :].astype(BF16)

    def make_target(s):
        loads[s].wait()
        for a in range(rt):
            for j in range(ct):
                block = (slice(a * tile, (a + 1) * tile), slice(j * tile, (j + 1) * tile))
                target[(s,) + block] = rating[(s,) + block].astype(F32) * scl[s, j, a]

    pl.semaphore_wait(barrier, greeted)

    sends = []

    def send(src, dst, one, two, where):
        copy = pltpu.make_async_remote_copy(
            src_ref=src, dst_ref=dst, send_sem=one, recv_sem=two, device_id=where, device_id_type=MESH
        )
        copy.start()
        return copy

    others = [{"user": lax.rem(w + d, nu)} for d in range(1, nu)]
    first = []
    for d, where in enumerate(others):
        first.append(send(vlow.at[mine], vlow.at[mine], vl_send.at[d], vl_recv.at[d], where))
    for d, where in enumerate(others):
        first.append(send(vfull.at[0, mine], vfull.at[0, mine], vf_send.at[d], vf_recv.at[d], where))
        first.append(send(cnt, cnt_in.at[d], c_send.at[d], c_recv.at[d], where))

    if mirrored:
        meta_ahead = send(meta, meta_in, m_send.at[2], m_recv.at[2], others[0])

    @pl.when(2 * z < layers)
    def _():
        upward()
        downward()

    @pl.when(2 * z >= layers)
    def _():
        downward()
        upward()

    signal(side_sem.at[0], beside[0])
    make_target(0)
    load_u.wait()

    for s in range(SUB):
        last = s == SUB - 1
        if s == 0:
            for copy in first[: nu - 1]:
                copy.wait_recv()
            for k in range(1, len(SIDES)):
                pl.semaphore_wait(side_sem.at[k - 1], 1)
                signal(side_sem.at[k], beside[k])
        v_low = vlow[...]

        both = mirrored and last
        if both:
            users_ahead.wait()

        def own_tile(a, j):
            return (
                pat[s, j, a].astype(F32),
                target[s, a * tile:(a + 1) * tile, j * tile:(j + 1) * tile],
            )

        def partner_tile(a, j):
            return (
                meta_in[meta_row(0, a, j), :],
                target_p[a * tile:(a + 1) * tile, j * tile:(j + 1) * tile],
            )

        def errors(low, a, tile_of):
            predicted = lax.dot_general(low, v_low, NT, preferred_element_type=F32)
            out = []
            for j in range(ct):
                weight, goal = tile_of(a, j)
                diff = predicted[:, j * tile:(j + 1) * tile] - goal
                out.append((weight * diff).astype(BF16))
            return jnp.concatenate(out, axis=1)

        sets = [(u, 0, own_tile)] + ([(u_p, rows, partner_tile)] if both else [])
        work = [(held, start, tile_of, a) for a in range(rt) for held, start, tile_of in sets]
        olds = [held[a * tile:(a + 1) * tile, :].astype(F32) for held, _, _, a in work]
        ones = [errors(old.astype(BF16), a, tile_of) for old, (_, _, tile_of, a) in zip(olds, work)]
        news = [
            old - user_step * (jnp.dot(one, v_low, preferred_element_type=F32) + penalty * old)
            for old, one in zip(olds, ones)
        ]
        lows = [new.astype(BF16) for new in news]
        seconds = [errors(low, a, tile_of) for low, (_, _, tile_of, a) in zip(lows, work)]
        for (held, start, _, a), new, low, second in zip(work, news, lows, seconds):
            place = slice(start + a * tile, start + (a + 1) * tile)
            ulow[place, :] = low
            err[place, :] = second
            if held is u:
                u[place, :] = new

        exchanged = []
        for j in range(ct):
            columns = slice(j * tile, (j + 1) * tile)
            deep = slice(0, len(sets) * rows)
            value = lax.dot_general(err[deep, columns], ulow[deep, :], TN, preferred_element_type=F32)
            part[columns, :] = value
            if both:
                continue
            psend[s, columns, :] = value.astype(BF16)
            for d, where in enumerate(others):
                exchanged.append(send(
                    psend.at[s, columns], precv.at[s, d, columns], p_send.at[s, d, j], p_recv.at[s, d, j], where
                ))

        if s == 0:
            pl.semaphore_wait(side_sem.at[len(SIDES) - 1], 1)
            for copy in first[nu - 1:]:
                copy.wait_recv()
            for copy in first:
                copy.wait_send()
            total = cnt[...]
            for d in range(nu - 1):
                total = total + cnt_in[d]
            cnt[...] = 1.0 / jnp.maximum(total, 1.0)
        if not last:
            forward = send(vfull.at[s], vfull.at[s + 1], fw_send.at[s], fw_recv.at[s], nxt)
            make_target(s + 1)
        if mirrored and s == SUB - 2:
            ratings_ahead.wait()
            meta_ahead.wait()
            for a in range(rt):
                for j in range(ct):
                    block = (slice(a * tile, (a + 1) * tile), slice(j * tile, (j + 1) * tile))
                    target_p[block] = rating_p[block].astype(F32) * meta_in[meta_row(1, a, j), :]

        squares = jnp.zeros((8, rank), F32)
        for j in range(ct):
            columns = slice(j * tile, (j + 1) * tile)
            for d in range(0 if both else nu - 1):
                exchanged[j * (nu - 1) + d].wait()
            total = part[columns, :]
            for d in range(0 if both else nu - 1):
                total = total + precv[s, d, columns, :].astype(F32)
            v_old = vfull[s, columns, :] if s == 0 else v_f32[columns, :]
            normed = total * cnt[pl.ds(s * ct + j, 1), :] + penalty * v_old
            squares = squares + jnp.sum((normed * normed).reshape(tile // 8, 8, rank), axis=0)
            if last:
                part[columns, :] = normed
            else:
                nsend[s, columns, :] = normed
        ss[s] = jnp.sum(squares, axis=0, keepdims=True)
        for d in range(1, nb):
            send(ss.at[s], ss_in.at[s, d - 1], s_send.at[s], s_recv.at[s], {"blk": lax.rem(g + d, nb)})
        if not last:
            ahead = send(nsend.at[s], nrecv.at[s], n_send.at[s], n_recv.at[s], nxt)

        if mirrored and s == 0:
            ratings_ahead = send(r_hbm.at[SUB - 1], rating_p, m_send.at[0], m_recv.at[0], others[0])
        if mirrored and s == SUB - 2:
            users_ahead = send(ulow.at[pl.ds(0, rows)], u_p, m_send.at[1], m_recv.at[1], others[0])
        wait_bytes(ss_in.at[s], s_recv.at[s])
        total = ss[s] + jnp.sum(ss_in[s], axis=0)
        mean = jnp.sum(total, axis=1, keepdims=True) / (nb * cols * rank)
        gain = item_step * lax.rsqrt(mean + epsilon)
        if not last:
            forward.wait()
            ahead.wait()
            fresh = vfull[s + 1] - gain * nrecv[s].astype(F32)
            v_f32[...] = fresh
            vlow[...] = fresh.astype(BF16)
            if s + 1 < SUB - 1:
                vfull[s + 1] = fresh
        else:
            vout[...] = v_f32[mine, :] - gain * part[mine, :]
    for s in range(SUB):
        wait_bytes(ss_in.at[s], s_send.at[s])


def hand_over(u, v, uo_hbm, vo_hbm, sem):
    copies = [pltpu.make_async_copy(v, vo_hbm, sem.at[0]), pltpu.make_async_copy(u, uo_hbm, sem.at[1])]
    for copy in copies:
        copy.start()
    for copy in copies:
        copy.wait()


def shards(user_factors, item_factors, ratings, tile_pattern, tile_scale):
    nb, nu = lax.axis_size("blk"), lax.axis_size("user")
    tile = ratings.shape[2] // tile_pattern.shape[2]
    rows, rank = user_factors.shape
    share = item_factors.shape[0]
    cols = ratings.shape[2]
    ct = cols // tile
    counts = -(-SUB * ct // 8) * 8
    marks = -(-2 * (rows // tile) * ct // 8) * 8
    dma = pltpu.SemaphoreType.DMA
    vmem = pltpu.VMEM
    hbm = pl.BlockSpec(memory_space=pl.ANY)
    whole = pl.BlockSpec(memory_space=pltpu.VMEM)
    smem = pl.BlockSpec(memory_space=pltpu.SMEM)
    users, items = pl.pallas_call(
        functools.partial(kernel, nb, nu, tile),
        out_shape=(vmem(user_factors.shape, F32), vmem(item_factors.shape, F32)),
        in_specs=[hbm, hbm, hbm, smem, smem],
        out_specs=(whole, whole),
        scratch_shapes=[
            vmem((SUB, rows, cols), BF16),
            vmem((SUB, rows, cols), F32),
            vmem((cols, rank), BF16),
            vmem((SUB, cols, rank), F32),
            vmem((cols, rank), F32),
            vmem((2 * rows, rank), BF16),
            vmem((2 * rows, cols), BF16),
            vmem((counts, rank), F32),
            vmem((nu - 1, counts, rank), F32),
            vmem((SUB, cols, rank), BF16),
            vmem((SUB, nu - 1, cols, rank), BF16),
            vmem((cols, rank), F32),
            vmem((SUB - 1, cols, rank), F32),
            vmem((SUB - 1, cols, rank), F32),
            vmem((SUB, 1, rank), F32),
            vmem((SUB, nb - 1, 1, rank), F32),
            dma(()), dma(()), dma((SUB,)),
            dma((nu - 1,)), dma((nu - 1,)),
            dma((nu - 1,)), dma((nu - 1,)),
            dma((nu - 1,)), dma((nu - 1,)),
            dma((SUB, nu - 1, ct)), dma((SUB, nu - 1, ct)),
            dma((SUB - 1,)), dma((SUB - 1,)),
            dma((SUB - 1,)), dma((SUB - 1,)),
            dma((SUB,)), dma((SUB,)),
            pltpu.SemaphoreType.REGULAR, pltpu.SemaphoreType.REGULAR,
            pltpu.SemaphoreType.REGULAR((len(SIDES),)),
            vmem((rows, cols), BF16),
            vmem((rows, cols), F32),
            vmem((rows, rank), BF16),
            vmem((marks, tile), F32),
            vmem((marks, tile), F32),
            dma((3,)), dma((3,)),
        ],
        compiler_params=pltpu.CompilerParams(collective_id=0, has_side_effects=True),
    )(user_factors, item_factors, ratings, jnp.swapaxes(tile_pattern, 1, 2), jnp.swapaxes(tile_scale, 1, 2))
    return pl.pallas_call(
        hand_over,
        out_shape=(
            jax.ShapeDtypeStruct(user_factors.shape, F32),
            jax.ShapeDtypeStruct(item_factors.shape, F32),
        ),
        in_specs=[whole, whole],
        out_specs=(hbm, hbm),
        scratch_shapes=[dma((2,))],
    )(pltpu.with_memory_space_constraint(users, pltpu.VMEM), pltpu.with_memory_space_constraint(items, pltpu.VMEM))


def solution(mesh):
    specs = (
        P(("blk", "user"), None),
        P(("blk", "user"), None),
        P(None, ("blk", "user"), None),
        P(None, ("blk", "user"), None),
        P(None, ("blk", "user"), None),
    )
    out_specs = (P(("blk", "user"), None), P(("blk", "user"), None))
    return jax.shard_map(shards, mesh=mesh, in_specs=specs, out_specs=out_specs, check_vma=False)
```
